32 devices in a mesh: replica: 4 (over y, core), shard: 8 (over z, x).
Axes of the slice: x: 2, y: 2, z: 4, core: 2. Of those that a mesh axis runs over, the one named last changes fastest.
Arguments:
- tokens: bfloat16 [32768, 768], P(('replica', 'shard')), may hold values from -6 to 6
- cotangent: bfloat16 [32768, 768], P(('replica', 'shard')), may hold values from -6 to 6
- seq_units: int32 [4, 16], P('replica'), may hold values from 16 to 112, as said below
- seq_order: int32 [4, 16], P('replica'), may hold values from 0 to 15, as said below
- share_start: int32 [4, 16], P('replica'), may hold values from 0 to 1023, as said below
- stacked_weight: bfloat16 [768, 2304], P('shard'), may hold values from -0.21875 to 0.21875
- query_bias: bfloat16 [768], P('shard'), may hold values from -3 to 3
- value_bias: bfloat16 [768], P('shard'), may hold values from -0.119628906 to 0.119628906
- out_weight: bfloat16 [768, 768], P('shard'), may hold values from -3.5 to 3.5
- out_bias: bfloat16 [768], P('shard'), may hold values from -1.1953125 to 1.1953125
- first_gain: bfloat16 [768], P('shard'), may hold values from 0.25 to 1.75
- first_shift: bfloat16 [768], P('shard'), may hold values from -1.796875 to 1.796875
- up_weight: bfloat16 [768, 3072], P('shard'), may hold values from -0.21875 to 0.21875
- up_bias: bfloat16 [3072], P('shard'), may hold values from -1.796875 to 1.796875
- down_weight: bfloat16 [3072, 768], P('shard'), may hold values from -0.15625 to 0.15625
- down_bias: bfloat16 [768], P('shard'), may hold values from -1.1953125 to 1.1953125
- second_gain: bfloat16 [768], P('shard'), may hold values from 0.25 to 1.75
- second_shift: bfloat16 [768], P('shard'), may hold values from -1.796875 to 1.796875
Outputs:
- layer_out: bfloat16 [32768, 768], P(('replica', 'shard'))
- input_grad: bfloat16 [32768, 768], P(('replica', 'shard'))
- stacked_grad: float32 [768, 2304], P('shard')
- query_bias_grad: float32 [768], P('shard')
- value_bias_grad: float32 [768], P('shard')
- out_weight_grad: float32 [768, 768], P('shard')
- out_bias_grad: float32 [768], P('shard')
- first_gain_grad: float32 [768], P('shard')
- first_shift_grad: float32 [768], P('shard')
- up_weight_grad: float32 [768, 3072], P('shard')
- up_bias_grad: float32 [3072], P('shard')
- down_weight_grad: float32 [3072, 768], P('shard')
- down_bias_grad: float32 [768], P('shard')
- second_gain_grad: float32 [768], P('shard')
- second_shift_grad: float32 [768], P('shard')
The draws below stay inside these ranges and needn't reach their ends.
Inputs may be any that keep to these rules, and one draw needn't show every extreme that they name: `seq_units`: lengths in units of 8 tokens. After the deal each device of a group owns exactly two sequences of at most 128 units together; one device owns exactly 128 units, a sequence of 112 units and one of 16. `seq_order`: each replica's row is a permutation of its 16 sequences. `share_start`: shares lie in sequence order without intersection, and the last sequence's share ends at row 1024.
All inputs are finite; a program needn't handle non-finite values.
Results may differ from the reference program's by a relative error of at most 0.02.
Values may be sent and summed in bfloat16 or wider, within the bound.
No kernel may reach another device: no remote copies, remote signals or barrier semaphores. Data moves between devices by JAX's collectives and lax.ppermute only.
A program may use at most 192 MiB of HBM per device.

```python
import functools
import math
import jax
import jax.numpy as jnp
from jax import lax

D = 768
HEADS = 12
HEAD_DIM = 64
FF = 3072
CAP = 1024
CU = 128
SEQS = 16
GROUPS = 4
TOKENS = 32768
N_SHARD = 8


def deal_all(key):

    def one_group(group_key):
        key_pairs, key_full, key_order, key_gaps = jax.random.split(group_key, 4)
        low_units = CU // 8
        high_units = 3 * CU // 8
        pair_units = jax.random.randint(key_pairs, (N_SHARD, 2), low_units, high_units + 1).astype(jnp.int32)
        full_dest = jax.random.randint(key_full, (), 0, N_SHARD)
        full_mask = (jnp.arange(N_SHARD) == full_dest)[:, None]
        top_pair = jnp.array([CU - CU // 8, CU // 8], jnp.int32)
        pair_units = jnp.where(full_mask, top_pair[None, :], pair_units)
        dealt_units = pair_units.reshape(-1)
        deal_order = jax.random.permutation(key_order, SEQS).astype(jnp.int32)
        seq_lengths = jnp.zeros((SEQS,), jnp.int32).at[deal_order].set(dealt_units)
        slack_rows = CAP - jnp.sum(seq_lengths)
        gap_weights = jax.random.randint(key_gaps, (SEQS,), 0, 4).astype(jnp.int32)
        weight_total = jnp.maximum(jnp.sum(gap_weights), 1)
        gap_rows = slack_rows * gap_weights // weight_total
        gap_rows = gap_rows.at[0].add(slack_rows - jnp.sum(gap_rows))
        starts = jnp.cumsum(gap_rows) + jnp.cumsum(seq_lengths) - seq_lengths
        return (seq_lengths, deal_order, starts.astype(jnp.int32))
    group_keys = jax.random.split(jax.random.fold_in(key, 11), GROUPS)
    return jax.vmap(one_group)(group_keys)


def draw_seq_units(key, part):
    return deal_all(key)[0]


def draw_seq_order(key, part):
    return deal_all(key)[1]


def draw_share_start(key, part):
    return deal_all(key)[2]


def block_levels(rng, extent, cuts, smallest, largest):
    loudness, own = 1.0, jax.random.fold_in(rng, 6)
    for dim, shards_of in cuts:
        heights = jnp.exp(jax.random.uniform(jax.random.fold_in(own, dim), (shards_of,), jnp.float32, smallest / len(cuts), largest / len(cuts)))
        loudness = loudness * jnp.repeat(heights, extent[dim] // shards_of).reshape([-1 if axis == dim else 1 for axis in range(len(extent))])
    return loudness


def normal_values(rng, dims, deviation, reach, shards=(), kind=jnp.bfloat16):
    result = jax.random.normal(rng, dims, jnp.float32) * deviation
    if len(shards) > 0:
        result = block_levels(rng, dims, shards, -0.22, 0.18) * result
    return jnp.clip(result, min=-reach, max=reach).astype(kind)


def setup_inputs(seed: int = 0) -> dict:
    keys = jax.random.split(jax.random.key(seed), 19)
    return {
        "tokens": normal_values(keys[0], (TOKENS, D), 1.0, 6.0, ((0, 32),)),
        "cotangent": normal_values(keys[1], (TOKENS, D), 1.0, 6.0, ((0, 32),)),
        "seq_units": draw_seq_units(jax.random.fold_in(keys[18], 71), 0),
        "seq_order": draw_seq_order(jax.random.fold_in(keys[18], 71), 0),
        "share_start": draw_share_start(jax.random.fold_in(keys[18], 71), 0),
        "stacked_weight": normal_values(keys[5], (D, 3 * D), D ** -0.5, 0.21875, ((0, 8),)),
        "query_bias": normal_values(keys[6], (D,), 0.5, 3.0, ((0, 8),)),
        "value_bias": normal_values(keys[7], (D,), 0.02, 0.119628906, ((0, 8),)),
        "out_weight": normal_values(keys[8], (D, D), (max(D // 256, 1)) ** -0.5, 3.5, ((0, 8),)),
        "out_bias": normal_values(keys[9], (D,), 0.2, 1.1953125, ((0, 8),)),
        "first_gain": jnp.clip(1.0 + 0.15 * jax.random.normal(keys[10], (D,), jnp.float32), 0.25, 1.75).astype(jnp.bfloat16),
        "first_shift": normal_values(keys[11], (D,), 0.3, 1.796875, ((0, 8),)),
        "up_weight": normal_values(keys[12], (D, FF), D ** -0.5, 0.21875, ((0, 8),)),
        "up_bias": normal_values(keys[13], (FF,), 0.3, 1.796875, ((0, 8),)),
        "down_weight": normal_values(keys[14], (FF, D), (FF // 2) ** -0.5, 0.15625, ((0, 8),)),
        "down_bias": normal_values(keys[15], (D,), 0.2, 1.1953125, ((0, 8),)),
        "second_gain": jnp.clip(1.0 + 0.15 * jax.random.normal(keys[16], (D,), jnp.float32), 0.25, 1.75).astype(jnp.bfloat16),
        "second_shift": normal_values(keys[17], (D,), 0.3, 1.796875, ((0, 8),)),
    }


EPSILON = 1e-12
MASKED = -1000000000.0
PRECISE = lax.Precision.HIGHEST

@jax.custom_vjp
def low(v):
    return lax.optimization_barrier(v.astype(jnp.bfloat16)).astype(jnp.float32)

@jax.custom_vjp
def low_back(v):
    return v

def low_keep(v):
    return (low(v), None)

def low_pass(kept, grad):
    return (grad,)

def back_keep(v):
    return (v, None)

def back_low(kept, grad):
    return (low(grad),)
low.defvjp(low_keep, low_pass)
low_back.defvjp(back_keep, back_low)

def product(left_side, right_side):
    return jnp.dot(left_side, right_side, precision=PRECISE, preferred_element_type=jnp.float32)

def layer_norm(values, norm_gain, norm_shift):
    center = values - lax.optimization_barrier(jnp.mean(values, -1, keepdims=True))
    spread = lax.optimization_barrier(jnp.mean(center * center, -1, keepdims=True))
    return center * lax.rsqrt(spread + EPSILON) * norm_gain + norm_shift

def routing(lengths, deal_order, starts, row_count, dest_count):
    total_seqs = lengths.shape[0]
    per_dest = row_count // dest_count
    labels = jnp.arange(total_seqs, dtype=jnp.int32)
    chosen = (deal_order[:, None] == labels[None, :]).astype(jnp.int32)
    dealt_len = lax.optimization_barrier(jnp.sum(chosen * lengths[None, :], 1)).reshape(dest_count, 2)
    dealt_start = lax.optimization_barrier(jnp.sum(chosen * starts[None, :], 1)).reshape(dest_count, 2)
    first_len = dealt_len[:, 0:1]
    second_len = dealt_len[:, 1:2]
    position = jnp.arange(per_dest, dtype=jnp.int32)[None, :]
    in_first = position < first_len
    in_second = jnp.logical_and(position >= first_len, position < first_len + second_len)
    source_rows = jnp.where(in_first, dealt_start[:, 0:1] + position, jnp.where(in_second, dealt_start[:, 1:2] + position - first_len, row_count)).astype(jnp.int32)
    segments = jnp.where(in_first, 0, jnp.where(in_second, 1, 2)).astype(jnp.int32)
    placed = lax.optimization_barrier(jnp.sum(chosen * labels[:, None], 0))
    earlier = jnp.concatenate([jnp.zeros((dest_count, 1), jnp.int32), first_len], 1).reshape(-1)
    offset = placed // 2 * per_dest + lax.optimization_barrier(jnp.sum(chosen * earlier[:, None], 0))
    row_index = jnp.arange(row_count, dtype=jnp.int32)[:, None]
    member = jnp.logical_and(row_index >= starts[None, :], row_index < (starts + lengths)[None, :])
    landing = lax.optimization_barrier(jnp.sum(jnp.where(member, offset[None, :] + row_index - starts[None, :], 0), 1))
    landing = (landing + jnp.where(jnp.any(member, 1), 0, dest_count * per_dest)).astype(jnp.int32)
    return (source_rows, segments, landing)

def block_layer(hidden_rows, seg_rows, weights):
    stacked, query_add, value_add, out_mat, out_add, gain_first, shift_first, up_mat, up_add, down_mat, down_add, gain_second, shift_second = weights
    row_count, feature_count = hidden_rows.shape
    biases = jnp.concatenate([query_add, jnp.zeros_like(query_add), value_add])
    projected = low(low_back(product(hidden_rows, stacked) + biases))
    queries = projected[:, :feature_count].reshape(row_count, HEADS, HEAD_DIM)
    key_rows = projected[:, feature_count:2 * feature_count].reshape(row_count, HEADS, HEAD_DIM)
    value_rows = projected[:, 2 * feature_count:].reshape(row_count, HEADS, HEAD_DIM)
    blocks = max(1, row_count // 512)
    block_rows = row_count // blocks
    score_scale = 1.0 / math.sqrt(HEAD_DIM)

    def per_block(block_items):
        query_blk, seg_query = block_items
        scores = score_scale * jnp.einsum('qhd,khd->hqk', query_blk, key_rows, precision=PRECISE)
        scores = low_back(jnp.where((seg_query[:, None] == seg_rows[None, :])[None], scores, MASKED))
        prob_low = low(jax.nn.softmax(scores, axis=-1))
        return jnp.einsum('hqk,khd->qhd', prob_low, value_rows, precision=PRECISE)
    mixture = lax.map(jax.checkpoint(per_block), (queries.reshape(blocks, block_rows, HEADS, HEAD_DIM), seg_rows.reshape(blocks, block_rows)))
    attended = low(low_back(mixture.reshape(row_count, feature_count)))
    branch = low_back(product(attended, out_mat) + out_add)
    normed_first = layer_norm(hidden_rows + branch, gain_first, shift_first)
    pre_act = low_back(product(low(normed_first), up_mat) + up_add)
    activated = low(jax.nn.gelu(pre_act, approximate=False))
    ffn_out = low_back(product(activated, down_mat) + down_add)
    return layer_norm(normed_first + ffn_out, gain_second, shift_second)

def deal_rows(values, source_rows):
    padded = jnp.concatenate([values, jnp.zeros((N_SHARD, 1, D), jnp.float32)], 1)
    picked = padded[:, source_rows.reshape(-1)]
    return picked.reshape(N_SHARD, N_SHARD, CU, D).transpose(1, 0, 2, 3).reshape(N_SHARD, CAP, D)

def return_rows(values, landing):
    arranged = values.reshape(N_SHARD, N_SHARD, CU, D).transpose(1, 0, 2, 3).reshape(N_SHARD, CAP, D)
    padded = jnp.concatenate([arranged, jnp.zeros((N_SHARD, 1, D), jnp.float32)], 1)
    return jnp.take(padded, landing, axis=1)

def reference(tokens, cotangent, seq_units, seq_order, share_start, stacked_weight, query_bias, value_bias, out_weight, out_bias, first_gain, first_shift, up_weight, up_bias, down_weight, down_bias, second_gain, second_shift):
    route = functools.partial(routing, row_count=CAP, dest_count=N_SHARD)
    source_rows, segments, landing = jax.vmap(route)(seq_units, seq_order, share_start)
    tokens_full = tokens.astype(jnp.float32).reshape(GROUPS, N_SHARD, CAP, D)
    grads_full = cotangent.astype(jnp.float32).reshape(GROUPS, N_SHARD, CAP, D)
    dealt_x = jax.vmap(deal_rows)(tokens_full, source_rows).reshape(GROUPS * N_SHARD, CAP, D)
    dealt_grad = jax.vmap(deal_rows)(grads_full, source_rows).reshape(GROUPS * N_SHARD, CAP, D)
    seg_rows = jnp.tile(segments[:, :, None, :], (1, 1, N_SHARD, 1)).reshape(GROUPS * N_SHARD, CAP)
    params = (stacked_weight.astype(jnp.float32), query_bias.astype(jnp.float32), value_bias.astype(jnp.float32), out_weight.astype(jnp.float32), out_bias.astype(jnp.float32), first_gain.astype(jnp.float32), first_shift.astype(jnp.float32), up_weight.astype(jnp.float32), up_bias.astype(jnp.float32), down_weight.astype(jnp.float32), down_bias.astype(jnp.float32), second_gain.astype(jnp.float32), second_shift.astype(jnp.float32))

    def forward(hidden_all, weights):

        def one_device(device_items):
            return jax.checkpoint(block_layer)(device_items[0], device_items[1], weights)
        return lax.map(one_device, (hidden_all, seg_rows))
    outputs, pullback = jax.vjp(forward, dealt_x, params)
    input_cot, weight_cots = pullback(dealt_grad)
    layer_out = jax.vmap(return_rows)(outputs.reshape(GROUPS, N_SHARD, CAP, D), landing)
    input_grad = jax.vmap(return_rows)(input_cot.reshape(GROUPS, N_SHARD, CAP, D), landing)
    return (layer_out.reshape(TOKENS, D).astype(jnp.bfloat16), input_grad.reshape(TOKENS, D).astype(jnp.bfloat16), weight_cots[0], weight_cots[1], weight_cots[2], weight_cots[3], weight_cots[4], weight_cots[5], weight_cots[6], weight_cots[7], weight_cots[8], weight_cots[9], weight_cots[10], weight_cots[11], weight_cots[12])
```

```python
import functools
import math

import jax
import jax.numpy as jnp
from jax import lax
from jax.experimental import pallas as pl
from jax.experimental.pallas import tpu as pltpu
from jax.sharding import PartitionSpec as P

HEADS = 12
HEAD_DIM = 64
EPSILON = 1e-12
PENALTY = -(2.0**30)
LANES = 128
SMALL_ROWS = 16

BF = jnp.bfloat16
F32 = jnp.float32


def dot(a, b):
    return jnp.dot(a, b, preferred_element_type=F32)


def dot_nt(a, b):
    return lax.dot_general(a, b, (((1,), (1,)), ((), ())), preferred_element_type=F32)


def dot_tn(a, b):
    return lax.dot_general(a, b, (((0,), (0,)), ((), ())), preferred_element_type=F32)


def routing(lengths, deal_order, starts, row_count, dest_count):
    total_seqs = lengths.shape[0]
    per_dest = row_count // dest_count
    labels = jnp.arange(total_seqs, dtype=jnp.int32)
    chosen = (deal_order[:, None] == labels[None, :]).astype(jnp.int32)
    dealt_len = jnp.sum(chosen * lengths[None, :], 1).reshape(dest_count, 2)
    dealt_start = jnp.sum(chosen * starts[None, :], 1).reshape(dest_count, 2)
    first_len = dealt_len[:, 0:1]
    second_len = dealt_len[:, 1:2]
    position = jnp.arange(per_dest, dtype=jnp.int32)[None, :]
    in_first = position < first_len
    in_second = jnp.logical_and(position >= first_len, position < first_len + second_len)
    source_rows = jnp.where(
        in_first,
        dealt_start[:, 0:1] + position,
        jnp.where(in_second, dealt_start[:, 1:2] + position - first_len, row_count),
    )
    segments = jnp.where(in_first, 0, jnp.where(in_second, 1, 2)).astype(jnp.int32)
    placed = jnp.sum(chosen * labels[:, None], 0)
    earlier = jnp.concatenate([jnp.zeros((dest_count, 1), jnp.int32), first_len], 1).reshape(-1)
    offset = placed // 2 * per_dest + jnp.sum(chosen * earlier[:, None], 0)
    row_index = jnp.arange(row_count, dtype=jnp.int32)[:, None]
    member = jnp.logical_and(row_index >= starts[None, :], row_index < (starts + lengths)[None, :])
    landing = jnp.sum(jnp.where(member, offset[None, :] + row_index - starts[None, :], 0), 1)
    landing = landing + jnp.where(jnp.any(member, 1), 0, dest_count * per_dest)
    return (source_rows, segments, landing)


def pick_kernel(rows_ref, values_ref, out_ref):
    wanted = rows_ref[...]
    columns = lax.broadcasted_iota(jnp.int32, (wanted.shape[0], values_ref.shape[0]), 1)
    chosen = jnp.where(columns == wanted, 1.0, 0.0).astype(BF)
    out_ref[...] = dot(chosen, values_ref[...]).astype(BF)


def pick_rows(values, rows):
    count, width = values.shape
    block = min(256, count)
    return pl.pallas_call(
        pick_kernel,
        grid=(count // block,),
        in_specs=[
            pl.BlockSpec((block, 1), lambda i: (i, 0)),
            pl.BlockSpec((count, width), lambda i: (0, 0)),
        ],
        out_specs=pl.BlockSpec((block, width), lambda i: (i, 0)),
        out_shape=jax.ShapeDtypeStruct((count, width), BF),
        cost_estimate=pl.CostEstimate(
            flops=2 * count * count * width, bytes_accessed=4 * count * width, transcendentals=0
        ),
        name="pick_rows",
    )(rows.reshape(count, 1), values)


def attend_kernel(q_ref, k_ref, v_ref, augq_ref, augk_ref, out_ref, aug_ref, kcat, vcat):
    rows = q_ref.shape[0]
    chunk = min(256, rows)
    lane = lax.broadcasted_iota(jnp.int32, (chunk, LANES), 1)
    low = lane < HEAD_DIM
    kcat[:, :LANES] = k_ref[...]
    kcat[:, LANES:] = augk_ref[...]
    vcat[:, :LANES] = v_ref[...]
    vcat[:, LANES:] = jnp.ones((rows, LANES), BF)
    scale = 1.0 / math.sqrt(HEAD_DIM)

    def one_chunk(i):
        here = pl.ds(i * chunk, chunk)
        q = q_ref[here, :] * scale
        seg = augq_ref[here, :]
        mixed = None
        aug = seg.astype(F32)
        for h in range(2):
            mine = low if h == 0 else jnp.logical_not(low)
            qcat = jnp.concatenate([jnp.where(mine, q, jnp.zeros_like(q)), seg], 1)
            scores = dot_nt(qcat, kcat[...])
            peak = jnp.max(scores, 1, keepdims=True)
            probs = jnp.exp(scores - peak).astype(BF)
            acc = dot(probs, vcat[...])
            total = acc[:, LANES:]
            part = acc[:, :LANES] / total
            mixed = part if h == 0 else jnp.where(low, mixed, part)
            lse = peak + jnp.log(total)
            high = lse.astype(BF).astype(F32)
            middle = (lse - high).astype(BF).astype(F32)
            rest = lse - high - middle
            base = 3 + 3 * h
            aug = jnp.where(lane == base, high, aug)
            aug = jnp.where(lane == base + 1, middle, aug)
            aug = jnp.where(lane == base + 2, rest, aug)
        out_ref[here, :] = mixed.astype(BF)
        aug_ref[here, :] = aug.astype(BF)

    for i in range(rows // chunk):
        one_chunk(i)


def attend(qkv, augq, augk):
    rows = qkv.shape[0]
    width = qkv.shape[1] // 3
    pairs = width // LANES
    whole = pl.BlockSpec((rows, LANES), lambda p: (0, 0))
    return pl.pallas_call(
        attend_kernel,
        grid=(pairs,),
        in_specs=[
            pl.BlockSpec((rows, LANES), lambda p: (0, p)),
            pl.BlockSpec((rows, LANES), lambda p: (0, pairs + p)),
            pl.BlockSpec((rows, LANES), lambda p: (0, 2 * pairs + p)),
            whole,
            whole,
        ],
        out_specs=[
            pl.BlockSpec((rows, LANES), lambda p: (0, p)),
            pl.BlockSpec((rows, LANES), lambda p: (0, p)),
        ],
        out_shape=[
            jax.ShapeDtypeStruct((rows, width), BF),
            jax.ShapeDtypeStruct((rows, width), BF),
        ],
        scratch_shapes=[pltpu.VMEM((rows, 2 * LANES), BF), pltpu.VMEM((rows, 2 * LANES), BF)],
        cost_estimate=pl.CostEstimate(
            flops=16 * rows * rows * width,
            bytes_accessed=10 * rows * width,
            transcendentals=rows * rows * HEADS,
        ),
        name="attend",
    )(qkv, qkv, qkv, augq, augk)


def attend_back_kernel(
    q_ref, k_ref, v_ref, aug_ref, augk_ref, a_ref, da_ref,
    dq_ref, dk_ref, dv_ref, qcat, dcat, kt, dqt,
):
    rows = q_ref.shape[0]
    chunk = min(256, rows)
    scale = 1.0 / math.sqrt(HEAD_DIM)
    lane = lax.broadcasted_iota(jnp.int32, (rows, LANES), 1)
    low = lane < HEAD_DIM
    q = q_ref[...] * scale
    grad = da_ref[...]
    aug = aug_ref[...]
    weighted = a_ref[...].astype(F32) * grad.astype(F32)
    zero = jnp.zeros_like(q)
    for h in range(2):
        mine = low if h == 0 else jnp.logical_not(low)
        other = 6 - 3 * h
        skip = jnp.logical_and(lane >= other, lane < other + 3)
        qcat[h, :, :LANES] = jnp.where(mine, q, zero)
        qcat[h, :, LANES:] = jnp.where(skip, zero, aug)
        inner = jnp.sum(jnp.where(mine, weighted, 0.0), 1, keepdims=True)
        high = inner.astype(BF).astype(F32)
        middle = (inner - high).astype(BF).astype(F32)
        rest = inner - high - middle
        split = jnp.where(lane == 0, high, jnp.where(lane == 1, middle, jnp.where(lane == 2, rest, 0.0)))
        dcat[h, :, :LANES] = jnp.where(mine, grad, zero)
        dcat[h, :, LANES:] = split.astype(BF)
    kt[...] = k_ref[...].T
    keyed = lax.broadcasted_iota(jnp.int32, (chunk, LANES), 1)
    minus = jnp.where(keyed < 3, -1.0, 0.0).astype(BF)
    low_key = keyed < HEAD_DIM
    for i in range(rows // chunk):
        here = pl.ds(i * chunk, chunk)
        kcat = jnp.concatenate([k_ref[here, :], augk_ref[here, :]], 1)
        vcat = jnp.concatenate([v_ref[here, :], minus], 1)
        keys = values = None
        for h in range(2):
            probs = jnp.exp(dot_nt(kcat, qcat[h]))
            slopes = dot_nt(vcat, dcat[h])
            low_probs = probs.astype(BF)
            low_slopes = (probs * slopes).astype(BF)
            dv = dot(low_probs, da_ref[...])
            dk = dot(low_slopes, q_ref[...])
            values = dv if h == 0 else jnp.where(low_key, values, dv)
            keys = dk if h == 0 else jnp.where(low_key, keys, dk)
            lines = pl.ds(h * HEAD_DIM, HEAD_DIM)
            part = dot(kt[lines, here], low_slopes)
            if i == 0:
                dqt[lines, :] = part
            else:
                dqt[lines, :] += part
        dv_ref[here, :] = values.astype(BF)
        dk_ref[here, :] = (keys * scale).astype(BF)
    dq_ref[...] = (dqt[...] * scale).T.astype(BF)


def attend_back(qkv, aug, augk, mixed, grad):
    rows = qkv.shape[0]
    width = qkv.shape[1] // 3
    pairs = width // LANES
    whole = pl.BlockSpec((rows, LANES), lambda p: (0, 0))
    mine = pl.BlockSpec((rows, LANES), lambda p: (0, p))
    return pl.pallas_call(
        attend_back_kernel,
        grid=(pairs,),
        in_specs=[
            mine,
            pl.BlockSpec((rows, LANES), lambda p: (0, pairs + p)),
            pl.BlockSpec((rows, LANES), lambda p: (0, 2 * pairs + p)),
            mine,
            whole,
            mine,
            mine,
        ],
        out_specs=[mine, mine, mine],
        out_shape=[jax.ShapeDtypeStruct((rows, width), BF)] * 3,
        scratch_shapes=[
            pltpu.VMEM((2, rows, 2 * LANES), BF),
            pltpu.VMEM((2, rows, 2 * LANES), BF),
            pltpu.VMEM((LANES, rows), BF),
            pltpu.VMEM((LANES, rows), F32),
        ],
        cost_estimate=pl.CostEstimate(
            flops=40 * rows * rows * width,
            bytes_accessed=18 * rows * width,
            transcendentals=rows * rows * HEADS,
        ),
        name="attend_back",
    )(qkv, qkv, qkv, aug, augk, mixed, grad)


def core_swap(x):
    size = lax.axis_size("replica")
    return lax.ppermute(x, "replica", [(r, r ^ 1) for r in range(size)])


def side_swap(x):
    size = lax.axis_size("replica")
    return lax.ppermute(x, "replica", [(r, r ^ 2) for r in range(size)])


def put(buffer, block, index, axis):
    starts = [jnp.int32(0)] * buffer.ndim
    starts[axis] = index
    return lax.dynamic_update_slice(buffer, jnp.expand_dims(block, axis), starts)


def spread(mine):
    rows, width = mine.shape
    half = rows // 2
    shards = lax.axis_size("shard")
    outer = shards // 2
    core = lax.axis_index("replica") % 2
    place = lax.axis_index("shard")
    near, far = place % 2, place // 2
    own = lax.dynamic_slice(mine, (core * half, 0), (half, width))
    line = put(jnp.zeros((outer, half, width), BF), own, far, 0)
    for k in range(1, outer):
        got = lax.ppermute(own, "shard", [(s, s ^ (2 * k)) for s in range(shards)])
        line = put(line, got, far ^ k, 0)
    got = lax.ppermute(line, "shard", [(s, s ^ 1) for s in range(shards)])
    plane = jnp.zeros((outer, 2, half, width), BF)
    plane = put(put(plane, line, near, 1), got, 1 - near, 1)
    got = core_swap(plane)
    full = jnp.zeros((outer, 2, 2, half, width), BF)
    full = put(put(full, plane, core, 2), got, 1 - core, 2)
    return full.reshape(shards, rows, width)


def share_sum(terms):
    shards, rows, width = terms.shape
    half = rows // 2
    core = lax.axis_index("replica") % 2
    kept = lax.dynamic_slice(terms, (0, core * half, 0), (shards, half, width))
    sent = lax.dynamic_slice(terms, (0, (1 - core) * half, 0), (shards, half, width))
    both = (kept.astype(F32) + core_swap(sent).astype(F32)).astype(BF)
    return both


def finish(part):
    half, width = part.shape
    low = part.astype(BF)
    total = low.astype(F32) + side_swap(low).astype(F32)
    other = core_swap(total)
    core = lax.axis_index("replica") % 2
    first = jnp.where(core == 0, total, other)
    second = jnp.where(core == 0, other, total)
    return jnp.concatenate([first, second], 0)


def small_block(parts, width):
    flat = jnp.concatenate(parts, -1)
    lead = flat.shape[:-1]
    pad = SMALL_ROWS * width - flat.shape[-1]
    flat = jnp.concatenate([flat, jnp.zeros(lead + (pad,), flat.dtype)], -1)
    return flat.reshape(lead + (SMALL_ROWS, width))


def columns(matrix, width):
    return [matrix[..., i * width : (i + 1) * width] for i in range(matrix.shape[-1] // width)]


def gelu_parts(u):
    rising = 0.5 * (1.0 + lax.erf(u * (1.0 / math.sqrt(2.0))))
    density = jnp.exp(-0.5 * u * u) * (1.0 / math.sqrt(2.0 * math.pi))
    return (u * rising).astype(BF), (rising + u * density).astype(BF)


def norm_parts(r):
    center = r - jnp.mean(r, -1, keepdims=True)
    spread_ = jnp.mean(center * center, -1, keepdims=True)
    scale = lax.rsqrt(spread_ + EPSILON)
    return center * scale, scale


def norm_back(dout, unit, scale, gain):
    e = dout * gain
    dr = (e - jnp.mean(e, -1, keepdims=True) - unit * jnp.mean(e * unit, -1, keepdims=True)) * scale
    return dr, jnp.sum(dout * unit, 0), jnp.sum(dout, 0)


def shards_body(
    tokens, cotangent, seq_units, seq_order, share_start,
    stacked_weight, query_bias, value_bias, out_weight, out_bias, first_gain, first_shift,
    up_weight, up_bias, down_weight, down_bias, second_gain, second_shift,
):
    row_count, width = tokens.shape
    dest_count = lax.axis_size("shard")
    replicas = lax.axis_size("replica")
    per_dest = row_count // dest_count
    my_index = lax.axis_index("shard")
    replica = lax.axis_index("replica")
    wrows = stacked_weight.shape[0]
    frows = down_weight.shape[0]

    source_rows, segments, landing = routing(
        seq_units[0], seq_order[0], share_start[0], row_count, dest_count
    )
    flat_rows = source_rows.reshape(-1)

    smalls = [query_bias, value_bias, out_bias, first_gain, first_shift, down_bias, second_gain, second_shift, up_bias]
    small = small_block(smalls, width)
    first_pack = jnp.concatenate(columns(stacked_weight, width) + [out_weight, small], 0)
    token_send = pick_rows(tokens, flat_rows)
    hidden = lax.all_to_all(
        token_send.reshape(dest_count, per_dest, width), "shard", split_axis=0, concat_axis=0, tiled=True
    ).reshape(row_count, width)
    gathered = spread(first_pack)
    part = lambda i: gathered[:, i * wrows : (i + 1) * wrows].reshape(dest_count * wrows, width)
    w_query, w_key, w_value, w_out = part(0), part(1), part(2), part(3)
    small_all = gathered[:, 4 * wrows :].reshape(dest_count, SMALL_ROWS * width)
    offsets = [wrows * i for i in range(9)]
    vec = lambda i, n=wrows: small_all[:, offsets[i] : offsets[i] + n].reshape(-1).astype(F32)
    query_add, value_add, out_add, gain_first, shift_first, down_add, gain_second, shift_second = [vec(i) for i in range(8)]
    up_add = vec(8, frows)

    quarter, fquarter = wrows // replicas, frows // replicas
    up_mine = lax.dynamic_slice(up_weight, (replica * quarter, 0), (quarter, up_weight.shape[1]))
    down_mine = lax.dynamic_slice(down_weight, (replica * fquarter, 0), (fquarter, width))
    second_pack = jnp.concatenate(columns(up_mine, width) + [down_mine], 0)
    second = lax.all_gather(second_pack, ("shard", "replica"), axis=0, tiled=False)
    ups = up_weight.shape[1] // width
    up_full = jnp.concatenate(
        [second[:, i * quarter : (i + 1) * quarter].reshape(dest_count * wrows, width) for i in range(ups)], 1
    )
    down_full = second[:, ups * quarter :].reshape(dest_count * frows, width)

    grad_send = pick_rows(cotangent, flat_rows)
    upstream = lax.all_to_all(
        grad_send.reshape(dest_count, per_dest, width), "shard", split_axis=0, concat_axis=0, tiled=True
    ).reshape(row_count, width).astype(F32)

    my_segments = lax.dynamic_index_in_dim(segments, my_index, 0, keepdims=False)
    seg_rows = jnp.tile(my_segments, dest_count)
    kinds = jnp.arange(LANES, dtype=jnp.int32)[None, :]
    augq = jnp.where(jnp.logical_and(seg_rows[:, None] == kinds, kinds < 3), 1.0, 0.0).astype(BF)
    augk = jnp.where(
        kinds < 3, jnp.where(seg_rows[:, None] == kinds, 0.0, PENALTY), jnp.where(kinds < 9, -1.0, 0.0)
    ).astype(BF)

    zero_add = jnp.zeros((width,), F32)
    w_stack = jnp.concatenate([w_query, w_key, w_value], 1)
    qkv = (dot(hidden, w_stack) + jnp.concatenate([query_add, zero_add, value_add])).astype(BF)
    mixed, aug = attend(qkv, augq, augk)
    unit1, scale1 = norm_parts(hidden.astype(F32) + dot(mixed, w_out) + out_add)
    normed = unit1 * gain_first + shift_first
    normed_low = normed.astype(BF)
    act, slope = gelu_parts(dot(normed_low, up_full) + up_add)
    unit2, scale2 = norm_parts(normed + dot(act, down_full) + down_add)
    result = (unit2 * gain_second + shift_second).astype(BF)

    d_r2, g_gain2, g_shift2 = norm_back(upstream, unit2, scale2, gain_second)
    d_z = d_r2.astype(BF)
    g_down = dot_tn(act, d_z)
    g_down_add = jnp.sum(d_z.astype(F32), 0)
    d_u = (dot_nt(d_z, down_full) * slope.astype(F32)).astype(BF)
    g_up = dot_tn(normed_low, d_u)
    g_up_add = jnp.sum(d_u.astype(F32), 0)
    d_r1, g_gain1, g_shift1 = norm_back(d_r2 + dot_nt(d_u, up_full), unit1, scale1, gain_first)
    d_o = d_r1.astype(BF)
    g_out = dot_tn(mixed, d_o)
    g_out_add = jnp.sum(d_o.astype(F32), 0)
    d_a = dot_nt(d_o, w_out).astype(BF)

    out_recv = lax.all_to_all(
        result.reshape(dest_count, per_dest, width), "shard", split_axis=0, concat_axis=0, tiled=True
    ).reshape(row_count, width)

    by_shard = lambda g: g.astype(BF).reshape(dest_count, -1, width)
    flat_small = lambda gs: small_block([g.astype(BF).reshape(dest_count, -1) for g in gs], width)
    first_terms = jnp.concatenate(
        [by_shard(g_down)]
        + [by_shard(c) for c in columns(g_up, width)]
        + [by_shard(g_out), flat_small([g_out_add, g_gain1, g_shift1, g_down_add, g_gain2, g_shift2, g_up_add])],
        1,
    )
    pair1 = share_sum(first_terms)
    sum1 = lax.psum_scatter(
        pair1.reshape(-1, width), "shard", scatter_dimension=0, tiled=True
    ).astype(F32)

    d_q, d_k, d_v = attend_back(qkv, aug, augk, mixed, d_a)
    g_q, g_k, g_v = dot_tn(hidden, d_q), dot_tn(hidden, d_k), dot_tn(hidden, d_v)
    g_q_add = jnp.sum(d_q.astype(F32), 0)
    g_v_add = jnp.sum(d_v.astype(F32), 0)
    d_x = (d_r1 + dot_nt(d_q, w_query) + dot_nt(d_k, w_key) + dot_nt(d_v, w_value)).astype(BF)
    input_recv = lax.all_to_all(
        d_x.reshape(dest_count, per_dest, width), "shard", split_axis=0, concat_axis=0, tiled=True
    ).reshape(row_count, width)

    second_terms = jnp.concatenate(
        [by_shard(g_q), by_shard(g_k), by_shard(g_v), flat_small([g_q_add, g_v_add])], 1
    )
    pair2 = share_sum(second_terms)
    got2 = lax.all_to_all(pair2, "shard", split_axis=0, concat_axis=0, tiled=True)
    sum2 = jnp.sum(got2.astype(F32), 0)

    final1 = finish(sum1)
    final2 = finish(sum2)

    layer_out = pick_rows(out_recv, landing)
    input_grad = pick_rows(input_recv, landing)

    up_parts = [final1[frows + i * wrows : frows + (i + 1) * wrows] for i in range(ups)]
    base = frows + ups * wrows
    tail1 = final1[base + wrows :].reshape(-1)
    tail2 = final2[3 * wrows :].reshape(-1)
    s1 = lambda i, n=wrows: tail1[i * wrows : i * wrows + n]
    return (
        layer_out,
        input_grad,
        jnp.concatenate([final2[i * wrows : (i + 1) * wrows] for i in range(3)], 1),
        tail2[:wrows],
        tail2[wrows : 2 * wrows],
        final1[base : base + wrows],
        s1(0),
        s1(1),
        s1(2),
        jnp.concatenate(up_parts, 1),
        s1(6, frows),
        final1[:frows],
        s1(3),
        s1(4),
        s1(5),
    )


def solution(mesh):
    rows = P(("replica", "shard"), None)
    table = P("replica", None)
    matrix = P("shard", None)
    vector = P("shard")
    weights = (
        matrix, vector, vector, matrix, vector, vector, vector,
        matrix, vector, matrix, vector, vector, vector,
    )
    return jax.shard_map(
        shards_body,
        mesh=mesh,
        in_specs=(rows, rows, table, table, table) + weights,
        out_specs=(rows, rows) + weights,
        check_vma=False,
    )
```
